128 devices in a mesh: row: 8 (over y_hi, z), col: 16 (over x, y_lo, core).
Axes of the slice: x: 4, y: 4 (y_hi: 2, y_lo: 2; y = y_hi * 2 + y_lo), z: 4, core: 2. Of those that a mesh axis runs over, the one named last changes fastest.
Arguments:
- activations: bfloat16 [1024, 28672], P(('row', 'col')), may hold values from -6 to 6
- gradients: bfloat16 [1024, 8192], P(('row', 'col')), may hold values from -6 to 6
- act_basis: bfloat16 [28672, 28672], P('col', 'row'), may hold values from -0.03125 to 0.03125
- grad_basis: bfloat16 [8192, 8192], P('row', 'col'), may hold values from -0.0625 to 0.0625
Outputs:
- correction: float32 [28672, 8192], P('row', 'col')
The draws below stay inside these ranges and needn't reach their ends.
All inputs are finite; a program needn't handle non-finite values.
Results may differ from the reference program's by a relative error of at most 0.0041.
Values may be sent and summed in bfloat16 or wider, within the bound.
No kernel may reach another device: no remote copies, remote signals or barrier semaphores. Data moves between devices by JAX's collectives and lax.ppermute only.
A program may use at most 128 MiB of HBM per device.

```python
import jax
import jax.numpy as jnp
from jax import lax

D = 8192
FF = 28672
SEQS = 2
LEN = 512
TOKENS = 1024


def level_of(key, shape, cuts, least, top_value):
    level = 1.0
    for position, blocks in cuts:
        heights = jax.random.uniform(jax.random.fold_in(jax.random.fold_in(key, 6), position), (blocks,), jnp.float32, least / len(cuts), top_value / len(cuts))
        level = level * jnp.repeat(jnp.exp(heights), shape[position] // blocks).reshape((-1,) + (1,) * (len(shape) - 1 - position))
    return level


def noise(rng, dims, spread, limit, shards=(), kind=jnp.bfloat16):
    gain = level_of(rng, dims, shards, -0.22, 0.18) if shards else 1.0
    values = jax.random.normal(rng, dims, jnp.float32) * spread * gain
    return jnp.minimum(jnp.maximum(values, -limit), limit).astype(kind)


def setup_inputs(seed: int = 0) -> dict:
    key_list = jax.random.split(jax.random.key(seed), 5)
    return {
        "activations": noise(key_list[0], (TOKENS, FF), 1.0, 6.0, ((0, 128),)),
        "gradients": noise(key_list[1], (TOKENS, D), 1.0, 6.0, ((0, 128),)),
        "act_basis": noise(key_list[2], (FF, FF), FF ** -0.5, 0.03125, ((0, 16), (1, 8))),
        "grad_basis": noise(key_list[3], (D, D), D ** -0.5, 0.0625, ((0, 8), (1, 16))),
    }


def reference(activations, gradients, act_basis, grad_basis):
    rot_grads = jnp.dot(gradients, grad_basis, preferred_element_type=jnp.float32).astype(jnp.bfloat16)
    blocks = act_basis.reshape(FF, 8, FF // 8).transpose(1, 0, 2)

    def one_block(columns):
        rot_acts = jnp.dot(activations, columns, preferred_element_type=jnp.float32).astype(jnp.bfloat16)
        total = jnp.zeros((FF // 8, D), jnp.float32)
        for seq in range(SEQS):
            left = rot_acts[seq * LEN:(seq + 1) * LEN]
            right = rot_grads[seq * LEN:(seq + 1) * LEN]
            grad_s = lax.dot_general(left, right, (((0,), (0,)), ((), ())), preferred_element_type=jnp.float32)
            total = total + grad_s * grad_s
        return total

    stacked = lax.map(one_block, blocks)
    return stacked.reshape(FF, D) * (1.0 / (SEQS * LEN))
```

```python
import functools

import jax
import jax.numpy as jnp
from jax import lax
from jax.experimental import pallas as pl
from jax.experimental.pallas import tpu as pltpu
from jax.sharding import Mesh
from jax.sharding import PartitionSpec as P

ROW = ("yh", "z")
COL = ("x", "yl", "c")
ALL = ROW + COL
BF = jnp.bfloat16
F32 = jnp.float32


def shift(v, axis, k):
    n = lax.axis_size(axis)
    return lax.ppermute(v, axis, [(i, (i + k) % n) for i in range(n)])


def rolled(v, k, dim):
    n = v.shape[dim]
    step = 1
    while step < n:
        turned = jnp.concatenate(
            [lax.slice_in_dim(v, step, n, axis=dim), lax.slice_in_dim(v, 0, step, axis=dim)], dim
        )
        v = jnp.where((k // step) % 2 == 1, turned, v)
        step *= 2
    return v


def ring(block, axis, half):
    down = shift(block, axis, 1)
    up = shift(block, axis, -1)
    far_a = shift(down[:half], axis, 1)
    far_b = shift(up[half:], axis, -1)
    return down, up, far_a, far_b


def dot(a, b):
    return jnp.dot(a, b, preferred_element_type=F32)


def last_kernel(side_ref, l0_ref, l1_ref, r_ref, *rest):
    o_ref = rest[-1]
    n = l0_ref.shape[0]
    dims = (((0,), (0,)), ((), ()))
    g0 = lax.dot_general(l0_ref[...], r_ref[:n], dims, preferred_element_type=F32)
    g1 = lax.dot_general(l1_ref[...], r_ref[n:], dims, preferred_element_type=F32)
    o_ref[...] = (g0 * g0 + g1 * g1) * (1.0 / (2 * n))


def last(side, l0, l1, r, before):
    n, width = l0.shape
    cols = r.shape[1]
    tile = 256
    steps = width // tile
    ins = [
        pl.BlockSpec((n, tile), lambda i, s: (0, i)),
        pl.BlockSpec((n, tile), lambda i, s: (0, i)),
        pl.BlockSpec((2 * n, cols), lambda i, s: (0, 0)),
    ]
    args = [l0, l1, r]
    alias = {}
    if before is not None:
        ins.append(pl.BlockSpec(memory_space=pl.ANY))
        args.append(before)
        alias = {4: 0}
    return pl.pallas_call(
        last_kernel,
        out_shape=jax.ShapeDtypeStruct((2 * width, cols), F32),
        grid_spec=pltpu.PrefetchScalarGridSpec(
            num_scalar_prefetch=1,
            grid=(steps,),
            in_specs=ins,
            out_specs=pl.BlockSpec((tile, cols), lambda i, s: (s[0] * steps + i, 0)),
        ),
        input_output_aliases=alias,
        cost_estimate=pl.CostEstimate(
            flops=4 * n * width * cols, bytes_accessed=4 * n * width + 4 * width * cols, transcendentals=0
        ),
        compiler_params=pltpu.CompilerParams(vmem_limit_bytes=24 * 2**20),
    )(side, *args)


def on_device(activations, gradients, act_basis, grad_basis):
    yh, z, x, yl, c = (lax.axis_index(a) for a in ALL)
    depth, width = act_basis.shape
    half = width // 2

    u_own = lax.dynamic_slice(act_basis, (0, c * half), (depth, half))
    u_sent = lax.dynamic_slice(act_basis, (0, (1 - c) * half), (depth, half))
    u_other = shift(u_sent, "c", 1)

    a = lax.all_to_all(activations, COL, split_axis=1, concat_axis=0, tiled=True)
    a = a.reshape(4, 2, 16, depth)
    a = rolled(a, x, 0)
    a = rolled(a, yl, 1)
    a = jnp.stack([a[0], a[3], a[1], a[2]]).transpose(1, 0, 2, 3).reshape(128, depth)
    a_swapped = shift(a, "yh", 1)

    g = lax.all_to_all(gradients, ROW, split_axis=1, concat_axis=0, tiled=True)
    gw = g.shape[1]
    g = g.reshape(2, 4, 8, gw)
    g = rolled(g, z, 1)
    g = rolled(g, yh, 0)
    g = jnp.stack([g[:, 0], g[:, 3], g[:, 1], g[:, 2]]).reshape(64, gw)

    def gather_acts(block):
        down, up, far0, far1 = ring(block, "z", 64)
        parts = []
        for e, far in ((0, far0), (1, far1)):
            rows = slice(64 * e, 64 * (e + 1))
            t = jnp.stack([block[rows], down[rows], up[rows], far])
            t = t.reshape(4, 4, 16, depth).transpose(1, 0, 2, 3).reshape(256, depth)
            parts.append(t)
        own = jnp.concatenate(parts, 0)
        return own, shift(own, "c", 1)

    def partial(own, other, rows):
        return dot(own[rows], u_own) + dot(other[rows], u_other)

    def reduce(own, other):
        theirs = partial(own, other, slice(256, 512)).astype(BF)
        got = shift(theirs, "yl", 1)
        mine = partial(own, other, slice(0, 256)) + got.astype(F32)
        m = [mine[64 * i : 64 * (i + 1)] for i in range(4)]
        f1 = shift(m[1].astype(BF), "x", -1)
        f2 = shift(m[2].astype(BF), "x", 1)
        f3 = shift(m[3].astype(BF), "x", 2)
        total = m[0] + f1.astype(F32) + f2.astype(F32) + f3.astype(F32)
        return total.astype(BF)

    def spread(v, n):
        pair = jnp.concatenate([v, shift(v, "yl", 1)], 0)
        down, up, far0, far1 = ring(pair, "x", n)
        return jnp.concatenate([pair, down, up, far0, far1], 0)

    g_own = spread(g, 64)
    g_other = shift(g_own, "c", 1)
    first = jnp.where(c == 0, g_own, g_other).reshape(8, 8, 8, gw)
    second = jnp.where(c == 0, g_other, g_own).reshape(8, 8, 8, gw)
    gm = jnp.stack([first, second], 2).transpose(1, 0, 2, 3, 4).reshape(1024, gw)
    pr = dot(gm, grad_basis).reshape(4, 256, -1)
    s = pr[0] + shift(pr[1], "z", -1) + shift(pr[2], "z", 1) + shift(pr[3], "z", 2)
    r = (s[:128] + shift(s[128:], "yh", 1)).astype(BF)
    pair = jnp.concatenate([r, shift(r, "yh", 1)], 0)
    zr = jnp.stack([pair, shift(pair, "z", 1), shift(pair, "z", -1), shift(pair, "z", 2)])
    rot = zr.reshape(4, 2, 8, 16, -1).transpose(1, 2, 0, 3, 4).reshape(1024, -1)

    ls = []
    for block in (a, a_swapped):
        own, other = gather_acts(block)
        mine = reduce(own, other)
        l_own = spread(mine, 64)
        ls.append((l_own, shift(l_own, "c", 1)))
    side = jnp.reshape(c, (1,)).astype(jnp.int32)
    out = last(side, ls[0][0], ls[1][0], rot, None)
    return last(1 - side, ls[0][1], ls[1][1], rot, out)


def solution(mesh):
    finer = Mesh(mesh.devices.reshape(2, 4, 4, 2, 2), ALL)
    return jax.shard_map(
        on_device,
        mesh=finer,
        in_specs=(P(ALL, None), P(ALL, None), P(COL, ROW), P(ROW, COL)),
        out_specs=P(ROW, COL),
        check_vma=False,
    )
```
